32 devices in a mesh: section: 4 (over z), row: 8 (over y, x, core).
Axes of the slice: x: 2, y: 2, z: 4, core: 2. Of those that a mesh axis runs over, the one named last changes fastest.
Arguments:
- features: bfloat16 [16, 16, 16, 192], P(None, 'row'), may hold values from -6 to 6
- norm_gain: float32 [4, 192], P('section'), may hold values from 0.5 to 1.5
- conv_weight: bfloat16 [4, 3, 3, 3, 192, 192], P('section'), may hold values from -0.078125 to 0.078125
- conv_bias: float32 [4, 192], P('section'), may hold values from -2.5 to 2.5
Outputs:
- decoded: bfloat16 [16, 16, 16, 192], P('section', 'row')
The draws below stay inside these ranges and needn't reach their ends.
All inputs are finite; a program needn't handle non-finite values.
Results may differ from the reference program's by a relative error of at most 0.03.
Values may be sent and summed in bfloat16 or wider, within the bound.
A program may use at most 64 MiB of HBM per device.

```python
import jax
import jax.numpy as jnp
from jax import lax

C = 192
COLS = 16
LAYERS = 4
FRAMES_ALL = 16
ROWS = 16


def block_levels(stream_key, dims, shards, low, top_value):
    gain, own = 1.0, jax.random.fold_in(stream_key, 6)
    for dim, shards_of in shards:
        steps = jnp.exp(jax.random.uniform(jax.random.fold_in(own, dim), (shards_of,), jnp.float32, low / len(shards), top_value / len(shards)))
        gain = gain * jnp.repeat(steps, dims[dim] // shards_of).reshape([-1 if axis == dim else 1 for axis in range(len(dims))])
    return gain


def centred(rng, extent, width, most, pieces=(), kind=jnp.bfloat16):
    result = width * jax.random.normal(rng, extent, jnp.float32)
    if pieces:
        result = result * block_levels(rng, extent, pieces, -0.22, 0.18)
    return jnp.clip(result, -most, most).astype(kind)


def setup_inputs(seed: int = 0) -> dict:
    splits = jax.random.split(jax.random.key(seed), 5)
    return {
        "features": centred(splits[0], (FRAMES_ALL, ROWS, COLS, C), 1.0, 6.0, ((1, 8),)),
        "norm_gain": jnp.clip(1.0 + 0.1 * jax.random.normal(splits[1], (LAYERS, C), jnp.float32), 0.5, 1.5),
        "conv_weight": centred(splits[2], (LAYERS, 3, 3, 3, C, C), (27 * C) ** -0.5, 0.078125, ((0, 4),)),
        "conv_bias": centred(splits[3], (LAYERS, C), 0.3, 2.5, ((0, 4),), jnp.float32),
    }


def reference(features, norm_gain, conv_weight, conv_bias):
    state = features
    for layer in range(LAYERS):
        wide = state.astype(jnp.float32)
        square = lax.optimization_barrier(jnp.mean(wide * wide, axis=-1, keepdims=True))
        normed = jax.nn.silu(wide * lax.rsqrt(square + 1e-06) * norm_gain[layer]).astype(jnp.bfloat16)
        padded = jnp.pad(normed, ((2, 0), (1, 1), (1, 1), (0, 0))).astype(jnp.float32)
        kernel = conv_weight[layer].astype(jnp.float32)
        conv = lax.conv_general_dilated(padded[None], kernel, (1, 1, 1), 'VALID', dimension_numbers=('NDHWC', 'DHWIO', 'NDHWC'), preferred_element_type=jnp.float32)[0]
        state = (wide + conv + conv_bias[layer]).astype(jnp.bfloat16)
    return state
```

```python
import functools

import jax
import jax.numpy as jnp
from jax import lax
from jax.experimental import pallas as pl
from jax.experimental.pallas import tpu as pltpu
from jax.sharding import PartitionSpec as P

FRAMES = 4
MESH = pl.DeviceIdType.MESH


def layer_kernel(
    sections, places, span, x_hbm, gain_ref, w_hbm, bias_ref, o_ref,
    own, above, below, taps, patches, result,
    load_sem, tap_sem, feature_send, send_sem, recv_sem, done_send, done_recv,
):
    frames, rows, cols, chans = own.shape
    turns = frames // span
    share = o_ref.shape[0]
    area = rows * cols
    layer = lax.axis_index("section")
    place = lax.axis_index("row")
    last = sections - 1
    has_above = place > 0
    has_below = place < places - 1
    is_first = layer == 0
    is_last = layer == last

    tap_copy = pltpu.make_async_copy(w_hbm, taps, tap_sem)
    tap_copy.start()
    own_copy = pltpu.make_async_copy(x_hbm, own, load_sem)

    @pl.when(is_first)
    def _():
        own_copy.start()

    barrier = pltpu.get_barrier_semaphore()

    def greet(section, row):
        pl.semaphore_signal(barrier, inc=1, device_id=(section, row), device_id_type=MESH)

    source = jnp.maximum(layer - 1, 0)

    @pl.when(jnp.logical_not(is_first))
    def _():
        greet(source, place)

    @pl.when(has_above)
    def _():
        greet(source, place - 1)

    @pl.when(has_below)
    def _():
        greet(source, place + 1)

    @pl.when(jnp.logical_not(is_last))
    def _():
        greet(last, place)

    beside = has_above.astype(jnp.int32) + has_below.astype(jnp.int32)
    first = is_first.astype(jnp.int32)
    final = is_last.astype(jnp.int32)
    pl.semaphore_wait(barrier, (1 - final) * (1 + beside) + first * beside + final * last)

    def send(src, dst, send_at, recv_at, section, row):
        return pltpu.make_async_remote_copy(
            src_ref=src, dst_ref=dst, send_sem=send_at, recv_sem=recv_at,
            device_id=(section, row), device_id_type=MESH,
        )

    def feature_above(turn):
        at = pl.ds(turn * span, span)
        return send(
            x_hbm.at[at, 0], below.at[at], feature_send.at[0, turn], recv_sem.at[2, turn], layer, place - 1
        )

    def feature_below(turn):
        at = pl.ds(turn * span, span)
        return send(
            x_hbm.at[at, rows - 1], above.at[at], feature_send.at[1, turn], recv_sem.at[1, turn], layer, place + 1
        )

    def next_own(turn):
        at = pl.ds(turn * span, span)
        return send(result.at[at], own.at[at], send_sem.at[0, turn], recv_sem.at[0, turn], layer + 1, place)

    def next_above(turn):
        at = pl.ds(turn * span, span)
        return send(
            result.at[at, 0], below.at[at], send_sem.at[2, turn], recv_sem.at[2, turn], layer + 1, place - 1
        )

    def next_below(turn):
        at = pl.ds(turn * span, span)
        return send(
            result.at[at, rows - 1], above.at[at], send_sem.at[1, turn], recv_sem.at[1, turn], layer + 1, place + 1
        )

    pieces = share // span

    def keep(turn):
        at = pl.ds(turn * span, span)
        part = lax.rem(turn, pieces)
        return send(
            result.at[at], o_ref.at[pl.ds(part * span, span)], done_send.at[turn], done_recv.at[part],
            turn // pieces, place,
        )

    @pl.when(is_first)
    def _():
        def begin(turn, carry):
            @pl.when(has_above)
            def _():
                feature_above(turn).start()

            @pl.when(has_below)
            def _():
                feature_below(turn).start()

            return carry

        lax.fori_loop(0, turns, begin, 0)

    empty = jnp.zeros(above.shape, above.dtype)

    @pl.when(jnp.logical_not(has_above))
    def _():
        above[...] = empty

    @pl.when(jnp.logical_not(has_below))
    def _():
        below[...] = empty

    patches[0 : 2 * area, :] = jnp.zeros((2 * area, patches.shape[1]), patches.dtype)
    gain = gain_ref[...]
    bias = bias_ref[...]
    wide = span * (rows + 2) * cols
    column = lax.rem(lax.broadcasted_iota(jnp.int32, (wide, chans), 0), cols)

    @pl.when(is_first)
    def _():
        own_copy.wait()

    def advance(turn, carry):
        at = pl.ds(turn * span, span)

        @pl.when(jnp.logical_not(is_first))
        def _():
            next_own(turn).wait_recv()

        @pl.when(has_above)
        def _():
            next_below(turn).wait_recv()

        @pl.when(has_below)
        def _():
            next_above(turn).wait_recv()

        state = own[at].astype(jnp.float32)
        high = above[at].astype(jnp.float32).reshape(span, 1, cols, chans)
        low = below[at].astype(jnp.float32).reshape(span, 1, cols, chans)
        block = jnp.concatenate([high, state, low], axis=1).reshape(wide, chans)
        square = jnp.mean(block * block, axis=-1, keepdims=True)
        scaled = block * lax.rsqrt(square + 1e-06) * gain
        normed = scaled / (1.0 + jnp.exp(-scaled))
        left = jnp.where(column == 0, 0.0, pltpu.roll(normed, 1, 0))
        right = jnp.where(column == cols - 1, 0.0, pltpu.roll(normed, wide - 1, 0))
        shifts = [
            value.astype(jnp.bfloat16).reshape(span, rows + 2, cols, chans)
            for value in (left, normed, right)
        ]
        stacked = jnp.concatenate(
            [
                shifts[dx][:, dy : dy + rows].reshape(span * area, chans)
                for dy in range(3)
                for dx in range(3)
            ],
            axis=-1,
        )
        base = turn * span * area
        patches[pl.ds(pl.multiple_of(base + 2 * area, area), span * area), :] = stacked
        total = state.reshape(span * area, chans) + bias

        @pl.when(turn == 0)
        def _():
            tap_copy.wait()

        for delay in range(3):
            window = patches[pl.ds(pl.multiple_of(base + delay * area, area), span * area), :]
            total = total + jnp.dot(window, taps[delay], preferred_element_type=jnp.float32)
        result[at] = total.astype(jnp.bfloat16).reshape(span, rows, cols, chans)

        @pl.when(jnp.logical_not(is_last))
        def _():
            next_own(turn).start()

            @pl.when(has_above)
            def _():
                next_above(turn).start()

            @pl.when(has_below)
            def _():
                next_below(turn).start()

        @pl.when(jnp.logical_and(is_last, turn // pieces < last))
        def _():
            keep(turn).start()

        return carry

    lax.fori_loop(0, turns, advance, 0)

    @pl.when(is_last)
    def _():
        o_ref[...] = result[pl.ds(frames - share, share)]

        def drain(turn, carry):
            keep(turn).wait_send()
            return carry

        lax.fori_loop(0, last * pieces, drain, 0)

    @pl.when(jnp.logical_not(is_last))
    def _():
        def drain(turn, carry):
            next_own(turn).wait_send()

            @pl.when(has_above)
            def _():
                next_above(turn).wait_send()

            @pl.when(has_below)
            def _():
                next_below(turn).wait_send()

            return carry

        lax.fori_loop(0, turns, drain, 0)

        def arrive(part, carry):
            keep(part).wait_recv()
            return carry

        lax.fori_loop(0, pieces, arrive, 0)

    @pl.when(is_first)
    def _():
        def drain(turn, carry):
            @pl.when(has_above)
            def _():
                feature_above(turn).wait_send()

            @pl.when(has_below)
            def _():
                feature_below(turn).wait_send()

            return carry

        lax.fori_loop(0, turns, drain, 0)


def on_device(features, norm_gain, conv_weight, conv_bias):
    sections = lax.axis_size("section")
    places = lax.axis_size("row")
    frames, rows, cols, chans = features.shape
    share = frames // sections
    span = min(FRAMES, share)
    turns = frames // span
    taps = conv_weight[0].reshape(3, 9 * chans, chans)
    vmem = pl.BlockSpec(memory_space=pltpu.VMEM)
    anywhere = pl.BlockSpec(memory_space=pl.ANY)
    dma = pltpu.SemaphoreType.DMA
    return pl.pallas_call(
        functools.partial(layer_kernel, sections, places, span),
        out_shape=jax.ShapeDtypeStruct((share, rows, cols, chans), jnp.bfloat16),
        in_specs=[anywhere, vmem, anywhere, vmem],
        out_specs=vmem,
        scratch_shapes=[
            pltpu.VMEM((frames, rows, cols, chans), jnp.bfloat16),
            pltpu.VMEM((frames, cols, chans), jnp.bfloat16),
            pltpu.VMEM((frames, cols, chans), jnp.bfloat16),
            pltpu.VMEM((3, 9 * chans, chans), jnp.bfloat16),
            pltpu.VMEM(((frames + 2) * rows * cols, 9 * chans), jnp.bfloat16),
            pltpu.VMEM((frames, rows, cols, chans), jnp.bfloat16),
            dma, dma, dma((2, turns)), dma((3, turns)), dma((3, turns)), dma((turns,)), dma((share // span,)),
        ],
        compiler_params=pltpu.CompilerParams(
            collective_id=0, has_side_effects=True, vmem_limit_bytes=40 * 1024 * 1024
        ),
    )(features, norm_gain, taps, conv_bias)


def solution(mesh):
    in_specs = (
        P(None, "row", None, None),
        P("section", None),
        P("section", None, None, None, None, None),
        P("section", None),
    )
    out_specs = P("section", "row", None, None)
    return jax.shard_map(
        on_device, mesh=mesh, in_specs=in_specs, out_specs=out_specs, check_vma=False
    )
```

```python
import functools

import jax
import jax.numpy as jnp
from jax import lax
from jax.experimental import pallas as pl
from jax.experimental.pallas import tpu as pltpu
from jax.sharding import PartitionSpec as P

FRAMES = 2
LANES = 128
MESH = pl.DeviceIdType.MESH


def layer_kernel(
    sections, places, span, x_hbm, gain_hbm, w_hbm, bias_hbm, o_ref,
    features, own, above, below, gain_ref, bias_ref, taps, patches, result, finished,
    load_sem, feature_send, edge_send, edge_recv, next_send, next_recv, done_send, done_recv,
):
    frames, rows, cols, chans = features.shape
    turns = frames // span
    share = o_ref.shape[0]
    pieces = share // span
    area = rows * cols
    layer = lax.axis_index("section")
    place = lax.axis_index("row")
    last = sections - 1
    has_above = place > 0
    has_below = place < places - 1
    is_first = layer == 0
    is_last = layer == last

    own_copy = pltpu.make_async_copy(x_hbm, features, load_sem.at[0])
    gain_copy = pltpu.make_async_copy(gain_hbm, gain_ref, load_sem.at[1])
    bias_copy = pltpu.make_async_copy(bias_hbm, bias_ref, load_sem.at[2])
    tap_copy = pltpu.make_async_copy(w_hbm, taps, load_sem.at[3])

    @pl.when(is_first)
    def _():
        own_copy.start()

    gain_copy.start()
    bias_copy.start()
    tap_copy.start()

    barrier = pltpu.get_barrier_semaphore()

    def greet(section, row):
        pl.semaphore_signal(barrier, inc=1, device_id=(section, row), device_id_type=MESH)

    source = jnp.maximum(layer - 1, 0)

    @pl.when(jnp.logical_not(is_first))
    def _():
        greet(source, place)

    @pl.when(has_above)
    def _():
        greet(source, place - 1)

    @pl.when(has_below)
    def _():
        greet(source, place + 1)

    @pl.when(jnp.logical_not(is_last))
    def _():
        greet(last, place)

    def pack(ref, at, value):
        upper, lower = value[:, 0], value[:, 1]
        ref[at, 0:cols, :] = upper[..., :LANES]
        ref[at, cols : 2 * cols, :] = jnp.concatenate([upper[..., LANES:], lower[..., LANES:]], axis=-1)
        ref[at, 2 * cols : 3 * cols, :] = lower[..., :LANES]

    empty = jnp.zeros(above.shape, above.dtype)

    @pl.when(jnp.logical_not(has_above))
    def _():
        above[...] = empty

    @pl.when(jnp.logical_not(has_below))
    def _():
        below[...] = empty

    patches[0 : 2 * area, :] = jnp.zeros((2 * area, patches.shape[1]), patches.dtype)
    wide = span * (rows + 2) * cols
    column = lax.rem(lax.broadcasted_iota(jnp.int32, (wide, chans), 0), cols)

    @pl.when(is_first)
    def _():
        own_copy.wait()
        pack(own, slice(None), features[...])

    beside = has_above.astype(jnp.int32) + has_below.astype(jnp.int32)
    first = is_first.astype(jnp.int32)
    final = is_last.astype(jnp.int32)
    pl.semaphore_wait(barrier, (1 - final) * (1 + beside) + first * beside + final * last)

    def stretch(turn):
        return pl.ds(turn * span, span)

    def send(src, dst, send_at, recv_at, section, row):
        return pltpu.make_async_remote_copy(
            src_ref=src, dst_ref=dst, send_sem=send_at, recv_sem=recv_at,
            device_id=(section, row), device_id_type=MESH,
        )

    def to_above(turn, src, sems, section):
        at = stretch(turn)
        return send(
            src.at[at, 0 : 2 * cols], below.at[at], sems.at[0, turn], edge_recv.at[0, turn], section, place - 1
        )

    def to_below(turn, src, sems, section):
        at = stretch(turn)
        return send(
            src.at[at, cols : 3 * cols], above.at[at], sems.at[1, turn], edge_recv.at[1, turn], section, place + 1
        )

    def own_above(turn):
        return to_above(turn, own, feature_send, layer)

    def own_below(turn):
        return to_below(turn, own, feature_send, layer)

    def next_above(turn):
        return to_above(turn, result, edge_send, layer + 1)

    def next_below(turn):
        return to_below(turn, result, edge_send, layer + 1)

    def to_next(turn):
        at = stretch(turn)
        return send(result.at[at], own.at[at], next_send.at[turn], next_recv.at[turn], layer + 1, place)

    def to_keeper(turn):
        part = lax.rem(turn, pieces)
        return send(
            finished.at[stretch(turn)], o_ref.at[stretch(part)], done_send.at[turn], done_recv.at[part],
            turn // pieces, place,
        )

    @pl.when(is_first)
    def _():
        def begin(turn, carry):
            @pl.when(has_above)
            def _():
                own_above(turn).start()

            @pl.when(has_below)
            def _():
                own_below(turn).start()

            return carry

        lax.fori_loop(0, turns, begin, 0)

    gain_copy.wait()
    bias_copy.wait()
    gain = gain_ref[...]
    bias = bias_ref[...]
    rest = chans - LANES

    def advance(turn, carry):
        at = stretch(turn)

        @pl.when(jnp.logical_not(is_first))
        def _():
            to_next(turn).wait_recv()

        @pl.when(has_above)
        def _():
            own_below(turn).wait_recv()

        @pl.when(has_below)
        def _():
            own_above(turn).wait_recv()

        def image_row(low, high):
            return jnp.concatenate([low, high], axis=-1).reshape(span, 1, cols, chans)

        held = own[at].astype(jnp.float32)
        over = above[at].astype(jnp.float32)
        under = below[at].astype(jnp.float32)
        mixed = held[:, cols : 2 * cols]
        upper = image_row(held[:, 0:cols], mixed[..., :rest])
        lower = image_row(held[:, 2 * cols :], mixed[..., rest:])
        high = image_row(over[:, cols:], over[:, 0:cols, rest:])
        low = image_row(under[:, 0:cols], under[:, cols:, :rest])
        block = jnp.concatenate([high, upper, lower, low], axis=1)
        state = block[:, 1:3].reshape(span * area, chans)
        block = block.reshape(wide, chans)
        square = jnp.mean(block * block, axis=-1, keepdims=True)
        scaled = block * lax.rsqrt(square + 1e-06) * gain
        normed = scaled / (1.0 + jnp.exp(-scaled))
        left = jnp.where(column == 0, 0.0, pltpu.roll(normed, 1, 0))
        right = jnp.where(column == cols - 1, 0.0, pltpu.roll(normed, wide - 1, 0))
        shifts = [
            value.astype(jnp.bfloat16).reshape(span, rows + 2, cols, chans)
            for value in (left, normed, right)
        ]
        stacked = jnp.concatenate(
            [
                shifts[dx][:, dy : dy + rows].reshape(span * area, chans)
                for dy in range(3)
                for dx in range(3)
            ],
            axis=-1,
        )
        base = turn * span * area
        patches[pl.ds(pl.multiple_of(base + 2 * area, area), span * area), :] = stacked
        total = state + bias

        @pl.when(turn == 0)
        def _():
            tap_copy.wait()

        for delay in range(3):
            window = patches[pl.ds(pl.multiple_of(base + delay * area, area), span * area), :]
            total = total + jnp.dot(window, taps[delay], preferred_element_type=jnp.float32)
        output = total.astype(jnp.bfloat16).reshape(span, rows, cols, chans)

        @pl.when(jnp.logical_not(is_last))
        def _():
            pack(result, at, output)
            to_next(turn).start()

            @pl.when(has_above)
            def _():
                next_above(turn).start()

            @pl.when(has_below)
            def _():
                next_below(turn).start()

        @pl.when(is_last)
        def _():
            finished[at] = output

            @pl.when(turn // pieces < last)
            def _():
                to_keeper(turn).start()

        return carry

    lax.fori_loop(0, turns, advance, 0)

    @pl.when(is_last)
    def _():
        o_ref[...] = finished[pl.ds(frames - share, share)]

        def drain(turn, carry):
            to_keeper(turn).wait_send()
            return carry

        lax.fori_loop(0, last * pieces, drain, 0)

    def drain(turn, carry):
        @pl.when(is_first & has_above)
        def _():
            own_above(turn).wait_send()

        @pl.when(is_first & has_below)
        def _():
            own_below(turn).wait_send()

        @pl.when(jnp.logical_not(is_last))
        def _():
            to_next(turn).wait_send()

            @pl.when(has_above)
            def _():
                next_above(turn).wait_send()

            @pl.when(has_below)
            def _():
                next_below(turn).wait_send()

        return carry

    lax.fori_loop(0, turns, drain, 0)

    @pl.when(jnp.logical_not(is_last))
    def _():
        def arrive(part, carry):
            to_keeper(part).wait_recv()
            return carry

        lax.fori_loop(0, pieces, arrive, 0)


def on_device(features, norm_gain, conv_weight, conv_bias):
    sections = lax.axis_size("section")
    places = lax.axis_size("row")
    frames, rows, cols, chans = features.shape
    share = frames // sections
    span = min(FRAMES, share)
    turns = frames // span
    taps = conv_weight[0].reshape(3, 9 * chans, chans)
    anywhere = pl.BlockSpec(memory_space=pl.ANY)
    dma = pltpu.SemaphoreType.DMA
    half = jnp.bfloat16
    return pl.pallas_call(
        functools.partial(layer_kernel, sections, places, span),
        out_shape=jax.ShapeDtypeStruct((share, rows, cols, chans), half),
        in_specs=[anywhere] * 4,
        out_specs=pl.BlockSpec(memory_space=pltpu.VMEM),
        scratch_shapes=[
            pltpu.VMEM((frames, rows, cols, chans), half),
            pltpu.VMEM((frames, 3 * cols, LANES), half),
            pltpu.VMEM((frames, 2 * cols, LANES), half),
            pltpu.VMEM((frames, 2 * cols, LANES), half),
            pltpu.VMEM(norm_gain.shape, jnp.float32),
            pltpu.VMEM(conv_bias.shape, jnp.float32),
            pltpu.VMEM((3, 9 * chans, chans), half),
            pltpu.VMEM(((frames + 2) * rows * cols, 9 * chans), half),
            pltpu.VMEM((frames, 3 * cols, LANES), half),
            pltpu.VMEM((frames, rows, cols, chans), half),
            dma((4,)), dma((2, turns)), dma((2, turns)), dma((2, turns)), dma((turns,)), dma((turns,)),
            dma((turns,)), dma((share // span,)),
        ],
        compiler_params=pltpu.CompilerParams(
            collective_id=0, has_side_effects=True, vmem_limit_bytes=60 * 1024 * 1024
        ),
    )(features, norm_gain, taps, conv_bias)


def solution(mesh):
    in_specs = (
        P(None, "row", None, None),
        P("section", None),
        P("section", None, None, None, None, None),
        P("section", None),
    )
    out_specs = P("section", "row", None, None)
    return jax.shard_map(
        on_device, mesh=mesh, in_specs=in_specs, out_specs=out_specs, check_vma=False
    )
```

```python
import functools

import jax
import jax.numpy as jnp
from jax import lax
from jax.experimental import pallas as pl
from jax.experimental.pallas import tpu as pltpu
from jax.sharding import PartitionSpec as P

FRAMES = 2
LANES = 128
MESH = pl.DeviceIdType.MESH


def layer_kernel(
    sections, places, span, x_hbm, gain_hbm, w_hbm, bias_hbm, o_ref,
    features, own, above, below, gain_ref, bias_ref, taps, patches, result, finished,
    load_sem, feature_send, edge_send, edge_recv, next_send, next_recv, done_send, done_recv,
):
    frames, rows, cols, chans = features.shape
    turns = frames // span
    share = o_ref.shape[0]
    pieces = share // span
    area = rows * cols
    layer = lax.axis_index("section")
    place = lax.axis_index("row")
    last = sections - 1
    has_above = place > 0
    has_below = place < places - 1
    is_first = layer == 0
    is_last = layer == last

    own_copy = pltpu.make_async_copy(x_hbm, features, load_sem.at[0])
    gain_copy = pltpu.make_async_copy(gain_hbm, gain_ref, load_sem.at[1])
    bias_copy = pltpu.make_async_copy(bias_hbm, bias_ref, load_sem.at[2])
    tap_copy = pltpu.make_async_copy(w_hbm, taps, load_sem.at[3])

    @pl.when(is_first)
    def _():
        own_copy.start()

    gain_copy.start()
    bias_copy.start()
    tap_copy.start()

    barrier = pltpu.get_barrier_semaphore()

    def greet(section, row):
        pl.semaphore_signal(barrier, inc=1, device_id=(section, row), device_id_type=MESH)

    source = jnp.maximum(layer - 1, 0)

    @pl.when(jnp.logical_not(is_first))
    def _():
        greet(source, place)

    @pl.when(has_above)
    def _():
        greet(source, place - 1)

    @pl.when(has_below)
    def _():
        greet(source, place + 1)

    @pl.when(jnp.logical_not(is_last))
    def _():
        greet(last, place)

    def pack(first, second):
        middle = jnp.concatenate([first[..., LANES:], second[..., LANES:]], axis=-1)
        return jnp.concatenate([first[..., :LANES], middle, second[..., :LANES]], axis=-2)

    def unpack(value):
        middle = value[..., cols : 2 * cols, :]
        rest = chans - LANES
        first = jnp.concatenate([value[..., 0:cols, :], middle[..., :rest]], axis=-1)
        second = jnp.concatenate([value[..., 2 * cols :, :], middle[..., rest:]], axis=-1)
        return jnp.stack([first, second])

    empty = jnp.zeros(above.shape, above.dtype)

    @pl.when(jnp.logical_not(has_above))
    def _():
        above[...] = empty

    @pl.when(jnp.logical_not(has_below))
    def _():
        below[...] = empty

    patches[:, 0:2] = jnp.zeros((3, 2) + patches.shape[2:], patches.dtype)
    wide = span * (rows + 2) * cols
    column = lax.rem(lax.broadcasted_iota(jnp.int32, (wide, chans), 0), cols)

    @pl.when(is_first)
    def _():
        own_copy.wait()
        value = features[...].reshape(turns, span, rows, cols, chans)
        own[...] = pack(value[:, 0], value[:, 1])

    beside = has_above.astype(jnp.int32) + has_below.astype(jnp.int32)
    first = is_first.astype(jnp.int32)
    final = is_last.astype(jnp.int32)
    pl.semaphore_wait(barrier, (1 - final) * (1 + beside) + first * beside + final * last)

    def stretch(turn):
        return pl.ds(turn * span, span)

    def send(src, dst, send_at, recv_at, section, row):
        return pltpu.make_async_remote_copy(
            src_ref=src, dst_ref=dst, send_sem=send_at, recv_sem=recv_at,
            device_id=(section, row), device_id_type=MESH,
        )

    def to_above(turn, src, sems, section):
        at = stretch(turn)
        return send(
            src.at[turn, 0], below.at[turn], sems.at[0, turn], edge_recv.at[0, turn], section, place - 1
        )

    def to_below(turn, src, sems, section):
        at = stretch(turn)
        return send(
            src.at[turn, rows - 1], above.at[turn], sems.at[1, turn], edge_recv.at[1, turn], section, place + 1
        )

    def own_above(turn):
        return to_above(turn, own, feature_send, layer)

    def own_below(turn):
        return to_below(turn, own, feature_send, layer)

    def next_above(turn):
        return to_above(turn, result, edge_send, layer + 1)

    def next_below(turn):
        return to_below(turn, result, edge_send, layer + 1)

    def to_next(turn):
        at = stretch(turn)
        return send(result.at[turn], own.at[turn], next_send.at[turn], next_recv.at[turn], layer + 1, place)

    def to_keeper(turn):
        part = lax.rem(turn, pieces)
        return send(
            finished.at[stretch(turn)], o_ref.at[stretch(part)], done_send.at[turn], done_recv.at[part],
            turn // pieces, place,
        )

    @pl.when(is_first)
    def _():
        def begin(turn, carry):
            @pl.when(has_above)
            def _():
                own_above(turn).start()

            @pl.when(has_below)
            def _():
                own_below(turn).start()

            return carry

        lax.fori_loop(0, turns, begin, 0)

    gain_copy.wait()
    bias_copy.wait()
    tap_copy.wait()
    gain = gain_ref[...]
    bias = bias_ref[...]

    def advance(turn, carry):
        at = stretch(turn)

        def mixed(delay):
            out = jnp.zeros((span * area, chans), jnp.float32)
            for dy in range(3):
                for dx in range(3):
                    window = patches[dx, pl.ds(turn * span + delay, span), dy : dy + rows].reshape(span * area, chans)
                    out = out + jnp.dot(window, taps[delay, dy, dx], preferred_element_type=jnp.float32)
            return out

        partial = mixed(0) + bias

        @pl.when(jnp.logical_not(is_first))
        def _():
            to_next(turn).wait_recv()

        @pl.when(has_above)
        def _():
            own_below(turn).wait_recv()

        @pl.when(has_below)
        def _():
            own_above(turn).wait_recv()

        block = jnp.concatenate([above[turn][None], own[turn], below[turn][None]], axis=0)
        block = unpack(block).astype(jnp.float32)
        state = block[:, 1:3].reshape(span * area, chans)
        block = block.reshape(wide, chans)
        square = jnp.mean(block * block, axis=-1, keepdims=True)
        scaled = block * lax.rsqrt(square + 1e-06) * gain
        normed = scaled / (1.0 + jnp.exp(-scaled))
        left = jnp.where(column == 0, 0.0, pltpu.roll(normed, 1, 0))
        right = jnp.where(column == cols - 1, 0.0, pltpu.roll(normed, wide - 1, 0))
        shifts = [
            value.astype(jnp.bfloat16).reshape(span, rows + 2, cols, chans)
            for value in (left, normed, right)
        ]
        for dx in range(3):
            patches[dx, pl.ds(turn * span + 2, span)] = shifts[dx]
        total = state + (partial + mixed(1) + mixed(2))
        output = total.astype(jnp.bfloat16).reshape(span, rows, cols, chans)

        @pl.when(jnp.logical_not(is_last))
        def _():
            result[turn] = pack(output[0], output[1])
            to_next(turn).start()

            @pl.when(has_above)
            def _():
                next_above(turn).start()

            @pl.when(has_below)
            def _():
                next_below(turn).start()

        @pl.when(is_last)
        def _():
            finished[at] = output

            @pl.when(turn // pieces < last)
            def _():
                to_keeper(turn).start()

        return carry

    lax.fori_loop(0, turns, advance, 0)

    @pl.when(is_last)
    def _():
        o_ref[...] = finished[pl.ds(frames - share, share)]

        def drain(turn, carry):
            to_keeper(turn).wait_send()
            return carry

        lax.fori_loop(0, last * pieces, drain, 0)

    def drain(turn, carry):
        @pl.when(is_first & has_above)
        def _():
            own_above(turn).wait_send()

        @pl.when(is_first & has_below)
        def _():
            own_below(turn).wait_send()

        @pl.when(jnp.logical_not(is_last))
        def _():
            to_next(turn).wait_send()

            @pl.when(has_above)
            def _():
                next_above(turn).wait_send()

            @pl.when(has_below)
            def _():
                next_below(turn).wait_send()

        return carry

    lax.fori_loop(0, turns, drain, 0)

    @pl.when(jnp.logical_not(is_last))
    def _():
        def arrive(part, carry):
            to_keeper(part).wait_recv()
            return carry

        lax.fori_loop(0, pieces, arrive, 0)


def on_device(features, norm_gain, conv_weight, conv_bias):
    sections = lax.axis_size("section")
    places = lax.axis_size("row")
    frames, rows, cols, chans = features.shape
    share = frames // sections
    span = FRAMES
    turns = frames // span
    taps = conv_weight[0]
    anywhere = pl.BlockSpec(memory_space=pl.ANY)
    dma = pltpu.SemaphoreType.DMA
    half = jnp.bfloat16
    return pl.pallas_call(
        functools.partial(layer_kernel, sections, places, span),
        out_shape=jax.ShapeDtypeStruct((share, rows, cols, chans), half),
        in_specs=[anywhere] * 4,
        out_specs=pl.BlockSpec(memory_space=pltpu.VMEM),
        scratch_shapes=[
            pltpu.VMEM((frames, rows, cols, chans), half),
            pltpu.VMEM((turns, rows, 3 * cols, LANES), half),
            pltpu.VMEM((turns, 3 * cols, LANES), half),
            pltpu.VMEM((turns, 3 * cols, LANES), half),
            pltpu.VMEM(norm_gain.shape, jnp.float32),
            pltpu.VMEM(conv_bias.shape, jnp.float32),
            pltpu.VMEM((3, 3, 3, chans, chans), half),
            pltpu.VMEM((3, frames + 2, rows + 2, cols, chans), half),
            pltpu.VMEM((turns, rows, 3 * cols, LANES), half),
            pltpu.VMEM((frames, rows, cols, chans), half),
            dma((4,)), dma((2, turns)), dma((2, turns)), dma((2, turns)), dma((turns,)), dma((turns,)),
            dma((turns,)), dma((share // span,)),
        ],
        compiler_params=pltpu.CompilerParams(
            collective_id=0, has_side_effects=True, vmem_limit_bytes=60 * 1024 * 1024
        ),
    )(features, norm_gain, taps, conv_bias)


def solution(mesh):
    in_specs = (
        P(None, "row", None, None),
        P("section", None),
        P("section", None, None, None, None, None),
        P("section", None),
    )
    out_specs = P("section", "row", None, None)
    return jax.shard_map(
        on_device, mesh=mesh, in_specs=in_specs, out_specs=out_specs, check_vma=False
    )
```

```python
import functools

import jax
import jax.numpy as jnp
from jax import lax
from jax.experimental import pallas as pl
from jax.experimental.pallas import tpu as pltpu
from jax.sharding import PartitionSpec as P

FRAMES = 2
LANES = 128
MESH = pl.DeviceIdType.MESH


def layer_kernel(
    sections, places, span, x_hbm, gain_hbm, w_hbm, bias_hbm, o_ref,
    features, own, above, below, gain_ref, bias_ref, taps, patches, result, finished,
    load_sem, feature_send, edge_send, edge_recv, next_send, next_recv, done_send, done_recv,
):
    frames, rows, cols, chans = features.shape
    turns = frames // span
    share = o_ref.shape[0]
    pieces = share // span
    area = rows * cols
    layer = lax.axis_index("section")
    place = lax.axis_index("row")
    last = sections - 1
    has_above = place > 0
    has_below = place < places - 1
    is_first = layer == 0
    is_last = layer == last

    own_copy = pltpu.make_async_copy(x_hbm, features, load_sem.at[0])
    gain_copy = pltpu.make_async_copy(gain_hbm, gain_ref, load_sem.at[1])
    bias_copy = pltpu.make_async_copy(bias_hbm, bias_ref, load_sem.at[2])
    tap_copy = pltpu.make_async_copy(w_hbm, taps, load_sem.at[3])

    @pl.when(is_first)
    def _():
        own_copy.start()

    gain_copy.start()
    bias_copy.start()
    tap_copy.start()

    barrier = pltpu.get_barrier_semaphore()

    def greet(section, row):
        pl.semaphore_signal(barrier, inc=1, device_id=(section, row), device_id_type=MESH)

    source = jnp.maximum(layer - 1, 0)

    @pl.when(jnp.logical_not(is_first))
    def _():
        greet(source, place)

    @pl.when(has_above)
    def _():
        greet(source, place - 1)

    @pl.when(has_below)
    def _():
        greet(source, place + 1)

    @pl.when(jnp.logical_not(is_last))
    def _():
        greet(last, place)

    def pack(first, second):
        middle = jnp.concatenate([first[..., LANES:], second[..., LANES:]], axis=-1)
        return jnp.concatenate([first[..., :LANES], middle, second[..., :LANES]], axis=-2)

    def unpack(value):
        middle = value[..., cols : 2 * cols, :]
        rest = chans - LANES
        first = jnp.concatenate([value[..., 0:cols, :], middle[..., :rest]], axis=-1)
        second = jnp.concatenate([value[..., 2 * cols :, :], middle[..., rest:]], axis=-1)
        return jnp.stack([first, second])

    empty = jnp.zeros(above.shape, above.dtype)

    @pl.when(jnp.logical_not(has_above))
    def _():
        above[...] = empty

    @pl.when(jnp.logical_not(has_below))
    def _():
        below[...] = empty

    patches[:, 0:2] = jnp.zeros((3, 2) + patches.shape[2:], patches.dtype)
    wide = span * (rows + 2) * cols
    column = lax.rem(lax.broadcasted_iota(jnp.int32, (wide, chans), 0), cols)

    @pl.when(is_first)
    def _():
        own_copy.wait()
        value = features[...].reshape(turns, span, rows, cols, chans)
        own[...] = pack(value[:, 0], value[:, 1])

    beside = has_above.astype(jnp.int32) + has_below.astype(jnp.int32)
    first = is_first.astype(jnp.int32)
    final = is_last.astype(jnp.int32)
    pl.semaphore_wait(barrier, (1 - final) * (1 + beside) + first * beside + final * last)

    def stretch(turn):
        return pl.ds(turn * span, span)

    def send(src, dst, send_at, recv_at, section, row):
        return pltpu.make_async_remote_copy(
            src_ref=src, dst_ref=dst, send_sem=send_at, recv_sem=recv_at,
            device_id=(section, row), device_id_type=MESH,
        )

    def to_above(turn, src, sems, section):
        at = stretch(turn)
        return send(
            src.at[turn, 0], below.at[turn], sems.at[0, turn], edge_recv.at[0, turn], section, place - 1
        )

    def to_below(turn, src, sems, section):
        at = stretch(turn)
        return send(
            src.at[turn, rows - 1], above.at[turn], sems.at[1, turn], edge_recv.at[1, turn], section, place + 1
        )

    def own_above(turn):
        return to_above(turn, own, feature_send, layer)

    def own_below(turn):
        return to_below(turn, own, feature_send, layer)

    def next_above(turn):
        return to_above(turn, result, edge_send, layer + 1)

    def next_below(turn):
        return to_below(turn, result, edge_send, layer + 1)

    def to_next(turn):
        at = stretch(turn)
        return send(result.at[turn], own.at[turn], next_send.at[turn], next_recv.at[turn], layer + 1, place)

    def to_keeper(turn):
        part = lax.rem(turn, pieces)
        return send(
            finished.at[stretch(turn)], o_ref.at[stretch(part)], done_send.at[turn], done_recv.at[part],
            turn // pieces, place,
        )

    @pl.when(is_first)
    def _():
        def begin(turn, carry):
            @pl.when(has_above)
            def _():
                own_above(turn).start()

            @pl.when(has_below)
            def _():
                own_below(turn).start()

            return carry

        lax.fori_loop(0, turns, begin, 0)

    gain_copy.wait()
    bias_copy.wait()
    tap_copy.wait()
    gain = gain_ref[...]
    bias = bias_ref[...]

    def advance(turn, carry):
        at = stretch(turn)

        def mixed(delay):
            out = jnp.zeros((span * area, chans), jnp.float32)
            for dy in range(3):
                for dx in range(3):
                    window = patches[dx, pl.ds(turn * span + delay, span), dy : dy + rows].reshape(span * area, chans)
                    out = out + jnp.dot(window, taps[delay, dy, dx], preferred_element_type=jnp.float32)
            return out

        partial = mixed(0) + bias

        @pl.when(jnp.logical_not(is_first))
        def _():
            to_next(turn).wait_recv()

        @pl.when(has_above)
        def _():
            own_below(turn).wait_recv()

        @pl.when(has_below)
        def _():
            own_above(turn).wait_recv()

        block = jnp.concatenate([above[turn][None], own[turn], below[turn][None]], axis=0)
        block = unpack(block).astype(jnp.float32)
        state = block[:, 1:3].reshape(span * area, chans)
        block = block.reshape(wide, chans)
        square = jnp.mean(block * block, axis=-1, keepdims=True)
        scaled = block * lax.rsqrt(square + 1e-06) * gain
        normed = scaled / (1.0 + jnp.exp(-scaled))
        left = jnp.where(column == 0, 0.0, pltpu.roll(normed, 1, 0))
        right = jnp.where(column == cols - 1, 0.0, pltpu.roll(normed, wide - 1, 0))
        shifts = [
            value.astype(jnp.bfloat16).reshape(span, rows + 2, cols, chans)
            for value in (left, normed, right)
        ]
        for dx in range(3):
            patches[dx, pl.ds(turn * span + 2, span)] = shifts[dx]
        total = state + (partial + mixed(1) + mixed(2))
        output = total.astype(jnp.bfloat16).reshape(span, rows, cols, chans)

        @pl.when(jnp.logical_not(is_last))
        def _():
            result[turn] = pack(output[0], output[1])
            @pl.when(has_above)
            def _():
                next_above(turn).start()

            @pl.when(has_below)
            def _():
                next_below(turn).start()

            to_next(turn).start()

        @pl.when(is_last)
        def _():
            finished[at] = output

            @pl.when(turn // pieces < last)
            def _():
                to_keeper(turn).start()

        return carry

    lax.fori_loop(0, turns, advance, 0)

    @pl.when(is_last)
    def _():
        o_ref[...] = finished[pl.ds(frames - share, share)]

        def drain(turn, carry):
            to_keeper(turn).wait_send()
            return carry

        lax.fori_loop(0, last * pieces, drain, 0)

    def drain(turn, carry):
        @pl.when(is_first & has_above)
        def _():
            own_above(turn).wait_send()

        @pl.when(is_first & has_below)
        def _():
            own_below(turn).wait_send()

        @pl.when(jnp.logical_not(is_last))
        def _():
            to_next(turn).wait_send()

            @pl.when(has_above)
            def _():
                next_above(turn).wait_send()

            @pl.when(has_below)
            def _():
                next_below(turn).wait_send()

        return carry

    lax.fori_loop(0, turns, drain, 0)

    @pl.when(jnp.logical_not(is_last))
    def _():
        def arrive(part, carry):
            to_keeper(part).wait_recv()
            return carry

        lax.fori_loop(0, pieces, arrive, 0)


def on_device(features, norm_gain, conv_weight, conv_bias):
    sections = lax.axis_size("section")
    places = lax.axis_size("row")
    frames, rows, cols, chans = features.shape
    share = frames // sections
    span = FRAMES
    turns = frames // span
    taps = conv_weight[0]
    anywhere = pl.BlockSpec(memory_space=pl.ANY)
    dma = pltpu.SemaphoreType.DMA
    half = jnp.bfloat16
    return pl.pallas_call(
        functools.partial(layer_kernel, sections, places, span),
        out_shape=jax.ShapeDtypeStruct((share, rows, cols, chans), half),
        in_specs=[anywhere] * 4,
        out_specs=pl.BlockSpec(memory_space=pltpu.VMEM),
        scratch_shapes=[
            pltpu.VMEM((frames, rows, cols, chans), half),
            pltpu.VMEM((turns, rows, 3 * cols, LANES), half),
            pltpu.VMEM((turns, 3 * cols, LANES), half),
            pltpu.VMEM((turns, 3 * cols, LANES), half),
            pltpu.VMEM(norm_gain.shape, jnp.float32),
            pltpu.VMEM(conv_bias.shape, jnp.float32),
            pltpu.VMEM((3, 3, 3, chans, chans), half),
            pltpu.VMEM((3, frames + 2, rows + 2, cols, chans), half),
            pltpu.VMEM((turns, rows, 3 * cols, LANES), half),
            pltpu.VMEM((frames, rows, cols, chans), half),
            dma((4,)), dma((2, turns)), dma((2, turns)), dma((2, turns)), dma((turns,)), dma((turns,)),
            dma((turns,)), dma((share // span,)),
        ],
        compiler_params=pltpu.CompilerParams(
            collective_id=0, has_side_effects=True, vmem_limit_bytes=60 * 1024 * 1024
        ),
    )(features, norm_gain, taps, conv_bias)


def solution(mesh):
    in_specs = (
        P(None, "row", None, None),
        P("section", None),
        P("section", None, None, None, None, None),
        P("section", None),
    )
    out_specs = P("section", "row", None, None)
    return jax.shard_map(
        on_device, mesh=mesh, in_specs=in_specs, out_specs=out_specs, check_vma=False
    )
```
